32 devices in a mesh: group: 4 (over x, core), shard: 8 (over z, y).
Axes of the slice: x: 2, y: 2, z: 4, core: 2. Of those that a mesh axis runs over, the one named last changes fastest.
Arguments:
- hidden: bfloat16 [8192, 768], P(('group', 'shard')), may hold values from -40 to 40
- out_grads: bfloat16 [5, 8192, 768], P(None, ('group', 'shard')), may hold values from -40 to 40
- global_inputs: bfloat16 [1024, 768], P(('group', 'shard')), may hold values from -40 to 40
- query_grads: bfloat16 [1024, 768], P(('group', 'shard')), may hold values from -40 to 40
- weight_grads: bfloat16 [6, 768, 768], P(None, 'shard'), may hold values from -48 to 48
- momentum: float32 [6, 768, 768], P(None, 'shard', 'group'), may hold values from -6 to 6
Outputs:
- new_momentum: float32 [6, 768, 768], P(None, 'shard', 'group')
The draws below stay inside these ranges and needn't reach their ends.
All inputs are finite; a program needn't handle non-finite values. Where the reference program divides by a largest or mean magnitude, that divisor is 1e-20 or more.
Results may differ from the reference program's by a relative error of at most 0.0018.
Values may be sent and summed in bfloat16 or wider, within the bound.
A program may use at most 128 MiB of HBM per device.

```python
import math
import jax
import jax.numpy as jnp
from jax import lax

D = 768
TOK_DEV = 256
GLOB_DEV = 32
ITERS = 3
TOKENS = 8192
GLOBALS = 1024
DEVICES = 32


def structured_rows(key, count_rows, columns):
    key_scale, key_load, key_common, key_noise = jax.random.split(key, 4)
    upper_scale = 4.0
    scales = jnp.exp(jax.random.uniform(key_scale, (columns,), jnp.float32, 0.0, math.log(upper_scale)))
    loadings = 0.1 * jax.random.normal(key_load, (4, columns), jnp.float32)
    common = jax.random.normal(key_common, (count_rows, 4), jnp.float32)
    fresh_noise = jax.random.normal(key_noise, (count_rows, columns), jnp.float32)
    mixed = fresh_noise + common[:, 0:1] * loadings[0] + common[:, 1:2] * loadings[1]
    mixed = mixed + common[:, 2:3] * loadings[2] + common[:, 3:4] * loadings[3]
    return jnp.clip(scales * mixed, -40.0, 40.0)


def draw_hidden(key, part):
    return structured_rows(jax.random.fold_in(key, 101), TOKENS, D).astype(jnp.bfloat16)


def draw_out_grads(key, part):
    return jnp.stack([structured_rows(jax.random.fold_in(key, 200 + member), TOKENS, D).astype(jnp.bfloat16) for member in range(5)])


def draw_global_inputs(key, part):
    return structured_rows(jax.random.fold_in(key, 301), GLOBALS, D).astype(jnp.bfloat16)


def draw_query_grads(key, part):
    return structured_rows(jax.random.fold_in(key, 401), GLOBALS, D).astype(jnp.bfloat16)


def level_of(key, extent, cuts, least, top_value):
    def one(dim, blocks):
        heights = jax.random.uniform(jax.random.fold_in(jax.random.fold_in(key, 6), dim), (blocks,), jnp.float32, least / len(cuts), top_value / len(cuts))
        return jnp.repeat(jnp.exp(heights), extent[dim] // blocks).reshape((-1,) + (1,) * (len(extent) - dim - 1))

    level = one(*cuts[0])
    for cut in cuts[1:]:
        level = level * one(*cut)
    return level


def gaussian(key, shape, width, bound, pieces=(), held_as=jnp.bfloat16):
    gain = level_of(key, shape, pieces, -0.22, 0.18) if pieces else 1.0
    values = jax.random.normal(key, shape, jnp.float32) * width * gain
    return jnp.minimum(jnp.maximum(values, -bound), bound).astype(held_as)


def setup_inputs(seed: int = 0) -> dict:
    key_list = jax.random.split(jax.random.key(seed), 7)
    hidden = draw_hidden(jax.random.fold_in(key_list[6], 71), 0)
    out_grads = draw_out_grads(jax.random.fold_in(key_list[6], 71), 0)
    global_inputs = draw_global_inputs(jax.random.fold_in(key_list[6], 71), 0)
    query_grads = draw_query_grads(jax.random.fold_in(key_list[6], 71), 0)
    weight_grads = gaussian(key_list[4], (6, D, D), 8.0, 48.0, ((1, 8),))
    momentum = gaussian(key_list[5], (6, D, D), 1.0, 6.0, ((1, 8), (2, 4)), jnp.float32)
    return dict(hidden=hidden, out_grads=out_grads, global_inputs=global_inputs, query_grads=query_grads, weight_grads=weight_grads, momentum=momentum)


PRECISE = lax.Precision.HIGHEST
DAMPING = 0.1
MOMENTUM = 0.9


def outer_sum(matrix_rows):
    widened = matrix_rows.astype(jnp.float32)
    return jnp.dot(widened.T, widened, precision=PRECISE)


def reference(hidden, out_grads, global_inputs, query_grads, weight_grads, momentum):
    devices = DEVICES
    hid_dev = hidden.reshape(devices, TOK_DEV, D)
    grad_dev = jnp.moveaxis(out_grads.reshape(5, devices, TOK_DEV, D), 1, 0)
    global_dev = global_inputs.reshape(devices, GLOB_DEV, D)
    query_dev = query_grads.reshape(devices, GLOB_DEV, D)

    def accumulate(summed, item):
        token_rows, grad_block, marked, queries = item
        partials = [outer_sum(token_rows), outer_sum(marked)]
        partials = partials + [outer_sum(grad_block[member]) for member in range(5)]
        partials = partials + [outer_sum(queries)]
        rounded = jnp.stack(partials).astype(jnp.bfloat16)
        rounded = lax.optimization_barrier(rounded)
        return summed + rounded.astype(jnp.float32), None

    initial = jnp.zeros((8, D, D), jnp.float32)
    summed, unused = lax.scan(accumulate, initial, (hid_dev, grad_dev, global_dev, query_dev))
    eye_full = jnp.eye(D, dtype=jnp.float32)
    inverses = []
    for factor in range(8):
        if factor == 1 or factor == 7:
            counted = float(GLOBALS)
        else:
            counted = float(TOKENS)
        covariance = summed[factor] / counted
        mean_diag = jnp.trace(covariance) / D
        matrix = covariance / mean_diag + DAMPING * eye_full
        row_limit = jnp.max(jnp.sum(jnp.abs(matrix), axis=1))
        approx = eye_full / row_limit
        for iteration in range(ITERS):
            approx = 2.0 * approx - jnp.dot(approx, jnp.dot(matrix, approx, precision=PRECISE), precision=PRECISE)
        inverses.append(approx)
    input_side = [0, 0, 0, 0, 0, 1]
    updated = []
    for weight in range(6):
        left_side = jnp.dot(inverses[2 + weight], weight_grads[weight].astype(jnp.float32), precision=PRECISE)
        precond = jnp.dot(left_side, inverses[input_side[weight]], precision=PRECISE)
        updated.append(MOMENTUM * momentum[weight] + precond)
    return jnp.stack(updated)
```

```python
import jax
import jax.numpy as jnp
from jax import lax
from jax.experimental import pallas as pl
from jax.experimental.pallas import tpu as pltpu
from jax.sharding import PartitionSpec as P

ITERS = 3


PRECISE = lax.Precision.HIGHEST
DAMPING = 0.1
MOMENTUM = 0.9


def broadcast(array, axis, root):
    mine = lax.axis_index(axis) == root
    return lax.psum(jnp.where(mine, array, jnp.zeros_like(array)), axis)


def outer_sum(matrix_rows):
    return lax.dot_general(
        matrix_rows, matrix_rows, (((0,), (0,)), ((), ())), preferred_element_type=jnp.float32
    )


def on_device(hidden, out_grads, global_inputs, query_grads, weight_grads, momentum):
    model_width = hidden.shape[1]
    group_size = lax.axis_size("group")
    shard_size = lax.axis_size("shard")
    per_group = 8 // group_size
    row_block = model_width // shard_size
    col_block = momentum.shape[2]
    shard_pos = lax.axis_index("shard")
    group_pos = lax.axis_index("group")
    devices = group_size * shard_size
    partials = [outer_sum(hidden), outer_sum(global_inputs)]
    partials = partials + [outer_sum(out_grads[member]) for member in range(5)]
    partials = partials + [outer_sum(query_grads)]
    stacked = jnp.stack([single.astype(jnp.bfloat16) for single in partials])
    summed = lax.psum_scatter(stacked, "group", scatter_dimension=0, tiled=True).astype(jnp.float32)
    factor_ids = group_pos * per_group + jnp.arange(per_group)
    is_global = (factor_ids == 1) | (factor_ids == 7)
    samp_total = float(hidden.shape[0] * devices)
    glob_total = float(global_inputs.shape[0] * devices)
    counted = jnp.where(is_global, glob_total, samp_total).astype(jnp.float32)
    factor_full = lax.psum(summed, "shard")
    covariance = factor_full / counted[:, None, None]
    mean_diag = jnp.trace(covariance, axis1=1, axis2=2) / model_width
    eye_full = jnp.eye(model_width, dtype=jnp.float32)
    matrix = covariance / mean_diag[:, None, None] + DAMPING * eye_full
    row_limit = jnp.max(jnp.sum(jnp.abs(matrix), axis=2), axis=1)
    approx = jnp.broadcast_to(eye_full, matrix.shape) / row_limit[:, None, None]
    for iteration in range(ITERS):
        product = jnp.einsum("kij,kjl->kil", matrix, approx, precision=PRECISE)
        approx = 2.0 * approx - jnp.einsum("kij,kjl->kil", approx, product, precision=PRECISE)
    own_rows = lax.dynamic_slice_in_dim(approx, shard_pos * row_block, row_block, 1)
    all_rows = lax.all_gather(own_rows, "group", axis=0, tiled=True)
    input_inv = jnp.stack(
        [broadcast(approx[factor % per_group], "group", factor // per_group) for factor in range(2)]
    )
    input_cols = lax.dynamic_slice_in_dim(input_inv, group_pos * col_block, col_block, 2)
    out_inverse = all_rows[2:8]
    initial = jnp.zeros(out_inverse.shape, jnp.float32)
    gathered = lax.all_gather(weight_grads, "shard", axis=1, tiled=True)
    columns = lax.slice_in_dim(out_inverse, 0, gathered.shape[1], axis=2)
    left_side = initial + jnp.einsum(
        "wrn,wnd->wrd", columns, gathered.astype(jnp.float32), precision=PRECISE
    )
    local_part = jnp.einsum("wrd,de->wre", left_side[0:5], input_cols[0], precision=PRECISE)
    global_part = jnp.dot(left_side[5], input_cols[1], precision=PRECISE)[None]
    return MOMENTUM * momentum + jnp.concatenate([local_part, global_part], axis=0)


MESH = pl.DeviceIdType.MESH
BLK = 256
HALF = 768
QUART = 192


def position():
    group, shard = lax.axis_index("group"), lax.axis_index("shard")
    core, x = lax.rem(group, 2), group // 2
    y, z = lax.rem(shard, 2), shard // 2
    return group, shard, core, x, y, z


def weight_of(core, y, x):
    return core * (2 + 2 * y + x) + (1 - core) * y * x


def greet(peers):
    barrier = pltpu.get_barrier_semaphore()
    for peer in peers:
        pl.semaphore_signal(barrier, inc=1, device_id=peer, device_id_type=MESH)
    pl.semaphore_wait(barrier, len(peers))


def add_rows(store, loads, rows):
    def step(i, carry):
        at = pl.multiple_of(i * 64, 64)
        total = loads[0](at).astype(jnp.float32)
        for load in loads[1:]:
            total = total + load(at).astype(jnp.float32)
        store(at, total.astype(jnp.bfloat16))
        return carry

    lax.fori_loop(0, rows // 64, step, 0)


def reduce_kernel(hid, ginp, outg, qry, wgr, cov, gfull, sendb, keep, rc, r2, r3, acc, zr,
                  cs, cr, as_, ar, bs, br, zs, zrs, fs, fr, gs, gr, lsem):
    group, shard, core, x, y, z = position()
    sibling = (group + 1 - 2 * core, shard)
    x_peer = ((1 - x) * 2 + core, shard)
    y_peer = (group, 2 * z + 1 - y)
    z_of = [lax.rem(z + dz, 4) for dz in range(4)]
    y_of = [y, 1 - y]
    shard_peers = [(dz, dy) for dz in range(4) for dy in range(2) if dz + dy > 0]
    greet([sibling, x_peer] + [(group, 2 * z_of[dz] + y_of[dy]) for dz, dy in shard_peers])

    def remote(src, dst, send, recv, device):
        return pltpu.make_async_remote_copy(
            src_ref=src, dst_ref=dst, send_sem=send, recv_sem=recv, device_id=device, device_id_type=MESH
        )

    def partial(factor, dst):
        if factor == 0:
            rows = hid[...]
        elif factor == 1:
            rows = ginp[...]
        elif factor == 7:
            rows = qry[...]
        else:
            rows = outg[factor - 2]
        at = 0
        for i in range(3):
            prod = lax.dot_general(
                rows[:, BLK * i:BLK * (i + 1)], rows[:, BLK * i:], (((0,), (0,)), ((), ())),
                preferred_element_type=jnp.float32,
            ).astype(jnp.bfloat16)
            for j in range(3 - i):
                dst[at * BLK:(at + 1) * BLK, :] = prod[:, BLK * j:BLK * (j + 1)]
                at += 1

    core_copies = [remote(sendb.at[j], rc.at[j], cs.at[j], cr.at[j], sibling) for j in range(4)]
    for owner in range(2):
        @pl.when(core != owner)
        def _():
            for j in range(4):
                partial(4 * owner + j, sendb.at[j])
                core_copies[j].start()

    grad_copies = []
    for k, (dz, dy) in enumerate(shard_peers):
        copy = remote(wgr.at[weight_of(core, y_of[dy], x)], gfull.at[shard], gs.at[k], gr.at[k],
                      (group, 2 * z_of[dz] + y_of[dy]))
        copy.start()
        grad_copies.append(copy)
    local = pltpu.make_async_copy(wgr.at[weight_of(core, y, x)], gfull.at[shard], lsem)
    local.start()
    for owner in range(2):
        @pl.when(core == owner)
        def _():
            for j in range(4):
                partial(4 * owner + j, keep.at[j])

    for j in range(4):
        core_copies[j].wait()

        def store(at, value, j=j):
            keep[j, pl.ds(at, 64), :] = value

        add_rows(store, [lambda at, j=j: keep[j, pl.ds(at, 64), :], lambda at, j=j: rc[j, pl.ds(at, 64), :]], 2 * HALF)

    first = [remote(keep.at[2 * t + 1 - x, pl.ds(0, HALF)], r2.at[0, t], as_.at[t], ar.at[t], x_peer) for t in range(2)]
    first += [remote(keep.at[2 * (1 - y) + t, pl.ds(HALF, HALF)], r2.at[1, t], as_.at[2 + t], ar.at[2 + t], y_peer)
              for t in range(2)]
    for copy in (first[0], first[2], first[1], first[3]):
        copy.start()
    for copy in first:
        copy.wait()
    passed = [2 * (1 - y) + x, 2 * y + 1 - x]
    other = [1 - y, 1 - x]
    same = [y, x]
    second = [remote(keep.at[passed[h], pl.ds(h * HALF, HALF)], r3.at[h], bs.at[h], br.at[h], [y_peer, x_peer][h])
              for h in range(2)]
    for h in range(2):
        def store(at, value, h=h):
            keep[passed[h], pl.ds(h * HALF + at, 64), :] = value

        add_rows(store, [lambda at, h=h: keep[passed[h], pl.ds(h * HALF + at, 64), :],
                         lambda at, h=h: r2[h, other[h], pl.ds(at, 64), :]], HALF)
        second[h].start()
    mine = 2 * y + x
    scatter, gather = [], []
    for h in range(2):
        second[h].wait()

        def store(at, value, h=h):
            acc[pl.ds(h * HALF + at, 64), :] = value

        add_rows(store, [lambda at, h=h: keep[mine, pl.ds(h * HALF + at, 64), :],
                         lambda at, h=h: r2[h, same[h], pl.ds(at, 64), :],
                         lambda at, h=h: r3[h, pl.ds(at, 64), :]], HALF)
        for dz in range(1, 4):
            copy = remote(acc.at[pl.ds(h * HALF + z_of[dz] * QUART, QUART)], zr.at[h, dz - 1],
                          zs.at[h, dz - 1], zrs.at[h, dz - 1], (group, 2 * z_of[dz] + y))
            copy.start()
            scatter.append(copy)
    for h in range(2):
        for copy in scatter[3 * h:3 * h + 3]:
            copy.wait()
        base = h * HALF + z * QUART

        def store(at, value, base=base):
            cov[pl.ds(base + at, 64), :] = value

        loads = [lambda at, base=base: acc[pl.ds(base + at, 64), :]]
        loads += [lambda at, h=h, d=d: zr[h, d, pl.ds(at, 64), :] for d in range(3)]
        add_rows(store, loads, QUART)
        for dz in range(1, 4):
            copy = remote(cov.at[pl.ds(base, QUART)], cov.at[pl.ds(base, QUART)],
                          fs.at[h, dz - 1], fr.at[h, dz - 1], (group, 2 * z_of[dz] + y))
            copy.start()
            gather.append(copy)
    for copy in gather + grad_copies:
        copy.wait()
    local.wait()


def spread_kernel(lch, xch, lout, xout, ls, lr, lsem):
    group, shard, core, x, y, z = position()
    offsets = [(dg, dy) for dg in range(4) for dy in range(2)]
    peers = [(lax.rem(group + dg, 4), lax.rem(y + dy, 2)) for dg, dy in offsets]
    greet([(pg, 2 * z + py) for pg, py in peers[1:]])
    weight = weight_of(core, y, x)

    def remote_left(k):
        pg, py = peers[k]
        return pltpu.make_async_remote_copy(
            src_ref=lch.at[py], dst_ref=lout.at[weight], send_sem=ls.at[k], recv_sem=lr.at[k],
            device_id=(pg, 2 * z + py), device_id_type=MESH)

    def remote_input(k):
        pg, py = peers[k]
        return pltpu.make_async_remote_copy(
            src_ref=xch.at[pg], dst_ref=xout.at[x], send_sem=ls.at[k], recv_sem=lr.at[k],
            device_id=(pg, 2 * z + py), device_id_type=MESH)

    @pl.when(core + y > 0)
    def _():
        for k in range(1, 8):
            remote_left(k).start()
        local = pltpu.make_async_copy(lch.at[y], lout.at[weight], lsem)
        local.start()
        local.wait()
        for k in range(1, 8):
            remote_left(k).wait_send()

    @pl.when(core + y == 0)
    def _():
        for k in range(1, 8):
            remote_input(k).start()
        local = pltpu.make_async_copy(xch.at[group], xout.at[x], lsem)
        local.start()
        local.wait()
        for k in range(1, 8):
            remote_input(k).wait_send()

    for k in range(1, 8):
        dg, dy = offsets[k]
        from_core = lax.rem(lax.rem(group + 4 - dg, 4), 2)
        from_y = lax.rem(y + dy, 2)

        @pl.when(from_core + from_y > 0)
        def _():
            remote_left(k).wait_recv()

        @pl.when(from_core + from_y == 0)
        def _():
            remote_input(k).wait_recv()


def split_high(values):
    high = lax.reduce_precision(values, 8, 7)
    return high.astype(jnp.bfloat16), (values - high).astype(jnp.bfloat16)


def fast_device(hidden, out_grads, global_inputs, query_grads, weight_grads, momentum):
    width = hidden.shape[1]
    group, shard, core, x, y, z = position()
    vmem = pl.BlockSpec(memory_space=pltpu.VMEM)
    dma = pltpu.SemaphoreType.DMA
    bf16 = jnp.bfloat16
    packed, gfull = pl.pallas_call(
        reduce_kernel,
        out_shape=(jax.ShapeDtypeStruct((2 * HALF, BLK), bf16), jax.ShapeDtypeStruct((8, 96, width), bf16)),
        in_specs=[vmem] * 5,
        out_specs=(vmem, vmem),
        scratch_shapes=[
            pltpu.VMEM((4, 2 * HALF, BLK), bf16),
            pltpu.VMEM((4, 2 * HALF, BLK), bf16),
            pltpu.VMEM((4, 2 * HALF, BLK), bf16),
            pltpu.VMEM((2, 2, HALF, BLK), bf16),
            pltpu.VMEM((2, HALF, BLK), bf16),
            pltpu.VMEM((2 * HALF, BLK), bf16),
            pltpu.VMEM((2, 3, QUART, BLK), bf16),
            dma((4,)), dma((4,)), dma((4,)), dma((4,)), dma((2,)), dma((2,)),
            dma((2, 3)), dma((2, 3)), dma((2, 3)), dma((2, 3)), dma((7,)), dma((7,)), dma,
        ],
        compiler_params=pltpu.CompilerParams(collective_id=0, has_side_effects=True, vmem_limit_bytes=48 * 2**20),
    )(hidden, global_inputs, out_grads, query_grads, weight_grads)
    blocks = packed.reshape(6, BLK, BLK).astype(jnp.float32)
    b00, b01, b02, b11, b12, b22 = [blocks[i] for i in range(6)]
    total = jnp.concatenate([
        jnp.concatenate([b00, b01, b02], axis=1),
        jnp.concatenate([b01.T, b11, b12], axis=1),
        jnp.concatenate([b02.T, b12.T, b22], axis=1),
    ], axis=0)
    devices = lax.axis_size("group") * lax.axis_size("shard")
    factor = 4 * core + 2 * y + x
    is_global = (factor == 1) | (factor == 7)
    counted = jnp.where(is_global, float(global_inputs.shape[0] * devices), float(hidden.shape[0] * devices))
    covariance = total / counted.astype(jnp.float32)
    eye = jnp.eye(width, dtype=jnp.float32)
    mean_diag = jnp.trace(covariance) / width
    matrix = covariance / mean_diag + DAMPING * eye
    row_limit = jnp.max(jnp.sum(jnp.abs(matrix), axis=1))
    a1 = matrix / row_limit

    def mul(left, right):
        return jnp.dot(left, right, precision=lax.Precision.HIGH)

    a2 = mul(a1, a1)
    a3 = mul(a1, a2)
    a4 = mul(a2, a2)
    rest = 4.0 * a2 - 6.0 * a1 - a3
    prod = 4.0 * a1 - 6.0 * a2 + 4.0 * a3 - a4
    inverse = (8.0 * eye + 2.0 * rest - 4.0 * prod - mul(rest, prod)) / row_limit
    diag = jnp.sum(inverse * eye, axis=1)
    off = (inverse * (1.0 - eye)).astype(bf16)
    grads = gfull.reshape(width, width)
    left = jnp.dot(lax.dynamic_slice_in_dim(off, z * 2 * 96, 2 * 96, 0), grads, preferred_element_type=jnp.float32)
    high, low = split_high(diag)

    def with_diag(rows, size):
        extra = jnp.zeros((rows.shape[0], 16, width), bf16)
        extra = extra.at[:, 0, :size].set(high_of(size)).at[:, 1, :size].set(low_of(size))
        return jnp.concatenate([rows, extra], axis=1)

    def high_of(size):
        if size == 96:
            return lax.dynamic_slice_in_dim(high, z * 192, 192, 0).reshape(2, 96)
        return high.reshape(4, 192)

    def low_of(size):
        if size == 96:
            return lax.dynamic_slice_in_dim(low, z * 192, 192, 0).reshape(2, 96)
        return low.reshape(4, 192)

    left_chunks = with_diag(left.astype(bf16).reshape(2, 96, width), 96)
    input_chunks = with_diag(off.reshape(4, 192, width), 192)
    left_all, input_all = pl.pallas_call(
        spread_kernel,
        out_shape=(jax.ShapeDtypeStruct((6, 112, width), bf16), jax.ShapeDtypeStruct((2, 208, width), bf16)),
        in_specs=[vmem] * 2,
        out_specs=(vmem, vmem),
        scratch_shapes=[dma((8,)), dma((8,)), dma],
        compiler_params=pltpu.CompilerParams(collective_id=1, has_side_effects=True, vmem_limit_bytes=32 * 2**20),
    )(left_chunks, input_chunks)
    out_diag = left_all[:, 96, :96].astype(jnp.float32) + left_all[:, 97, :96].astype(jnp.float32)
    left_side = out_diag[:, :, None] * weight_grads.astype(jnp.float32) + left_all[:, :96].astype(jnp.float32)
    in_diag = input_all[:, 192, :192].astype(jnp.float32) + input_all[:, 193, :192].astype(jnp.float32)
    columns = lax.dynamic_slice_in_dim(left_side, group * 192, 192, 2)
    narrow = left_side.astype(bf16)

    def right(rows, which):
        return lax.dot_general(rows, input_all[which, :192], (((rows.ndim - 1,), (1,)), ((), ())),
                               preferred_element_type=jnp.float32)

    step = jnp.concatenate([
        right(narrow[0:5], 0) + columns[0:5] * in_diag[0],
        (right(narrow[5], 1) + columns[5] * in_diag[1])[None],
    ], axis=0)
    return MOMENTUM * momentum + step


def solution(mesh):
    placed = (
        P(("group", "shard"), None),
        P(None, ("group", "shard"), None),
        P(("group", "shard"), None),
        P(("group", "shard"), None),
        P(None, "shard", None),
        P(None, "shard", "group"),
    )
    pairs = mesh.shape["group"] == 4 and mesh.shape["shard"] == 8
    return jax.shard_map(
        fast_device if pairs else on_device, mesh=mesh, in_specs=placed, out_specs=P(None, "shard", "group"), check_vma=False
    )
```

```python
import jax
import jax.numpy as jnp
from jax import lax
from jax.experimental import pallas as pl
from jax.experimental.pallas import tpu as pltpu
from jax.sharding import PartitionSpec as P

ITERS = 3


PRECISE = lax.Precision.HIGHEST
DAMPING = 0.1
MOMENTUM = 0.9


def broadcast(array, axis, root):
    mine = lax.axis_index(axis) == root
    return lax.psum(jnp.where(mine, array, jnp.zeros_like(array)), axis)


def outer_sum(matrix_rows):
    return lax.dot_general(
        matrix_rows, matrix_rows, (((0,), (0,)), ((), ())), preferred_element_type=jnp.float32
    )


def on_device(hidden, out_grads, global_inputs, query_grads, weight_grads, momentum):
    model_width = hidden.shape[1]
    group_size = lax.axis_size("group")
    shard_size = lax.axis_size("shard")
    per_group = 8 // group_size
    row_block = model_width // shard_size
    col_block = momentum.shape[2]
    shard_pos = lax.axis_index("shard")
    group_pos = lax.axis_index("group")
    devices = group_size * shard_size
    partials = [outer_sum(hidden), outer_sum(global_inputs)]
    partials = partials + [outer_sum(out_grads[member]) for member in range(5)]
    partials = partials + [outer_sum(query_grads)]
    stacked = jnp.stack([single.astype(jnp.bfloat16) for single in partials])
    summed = lax.psum_scatter(stacked, "group", scatter_dimension=0, tiled=True).astype(jnp.float32)
    factor_ids = group_pos * per_group + jnp.arange(per_group)
    is_global = (factor_ids == 1) | (factor_ids == 7)
    samp_total = float(hidden.shape[0] * devices)
    glob_total = float(global_inputs.shape[0] * devices)
    counted = jnp.where(is_global, glob_total, samp_total).astype(jnp.float32)
    factor_full = lax.psum(summed, "shard")
    covariance = factor_full / counted[:, None, None]
    mean_diag = jnp.trace(covariance, axis1=1, axis2=2) / model_width
    eye_full = jnp.eye(model_width, dtype=jnp.float32)
    matrix = covariance / mean_diag[:, None, None] + DAMPING * eye_full
    row_limit = jnp.max(jnp.sum(jnp.abs(matrix), axis=2), axis=1)
    approx = jnp.broadcast_to(eye_full, matrix.shape) / row_limit[:, None, None]
    for iteration in range(ITERS):
        product = jnp.einsum("kij,kjl->kil", matrix, approx, precision=PRECISE)
        approx = 2.0 * approx - jnp.einsum("kij,kjl->kil", approx, product, precision=PRECISE)
    own_rows = lax.dynamic_slice_in_dim(approx, shard_pos * row_block, row_block, 1)
    all_rows = lax.all_gather(own_rows, "group", axis=0, tiled=True)
    input_inv = jnp.stack(
        [broadcast(approx[factor % per_group], "group", factor // per_group) for factor in range(2)]
    )
    input_cols = lax.dynamic_slice_in_dim(input_inv, group_pos * col_block, col_block, 2)
    out_inverse = all_rows[2:8]
    initial = jnp.zeros(out_inverse.shape, jnp.float32)
    gathered = lax.all_gather(weight_grads, "shard", axis=1, tiled=True)
    columns = lax.slice_in_dim(out_inverse, 0, gathered.shape[1], axis=2)
    left_side = initial + jnp.einsum(
        "wrn,wnd->wrd", columns, gathered.astype(jnp.float32), precision=PRECISE
    )
    local_part = jnp.einsum("wrd,de->wre", left_side[0:5], input_cols[0], precision=PRECISE)
    global_part = jnp.dot(left_side[5], input_cols[1], precision=PRECISE)[None]
    return MOMENTUM * momentum + jnp.concatenate([local_part, global_part], axis=0)


MESH = pl.DeviceIdType.MESH
BLK = 256
HALF = 768
PARTS = 2
SUB = HALF // PARTS
ZROWS = SUB // 4
STEP = 32


def position():
    group, shard = lax.axis_index("group"), lax.axis_index("shard")
    core, x = lax.rem(group, 2), group // 2
    y, z = lax.rem(shard, 2), shard // 2
    return group, shard, core, x, y, z


def weight_of(core, y, x):
    return core * (2 + 2 * y + x) + (1 - core) * y * x


def greet(peers):
    barrier = pltpu.get_barrier_semaphore()
    for peer in peers:
        pl.semaphore_signal(barrier, inc=1, device_id=peer, device_id_type=MESH)
    pl.semaphore_wait(barrier, len(peers))


def add_rows(store, loads, rows):
    def step(i, carry):
        at = pl.multiple_of(i * STEP, STEP)
        total = loads[0](at).astype(jnp.float32)
        for load in loads[1:]:
            total = total + load(at).astype(jnp.float32)
        store(at, total.astype(jnp.bfloat16))
        return carry

    lax.fori_loop(0, rows // STEP, step, 0)


def step_kernel(hid, ginp, outg, qry, wgr, lout, xout, dall, sendb, keep, rc, r2, r3, acc, zr,
                cov, gfull, off_a, off_b, off_r, off_y, nar_a, nar_b, nar_r, nar_y, left,
                cs, cr, as_, ar, bs, br, zs, zrs, fs, fr, gs, gr, ls, lr, ds_, dr, lsem, lsem2, dsem):
    group, shard, core, x, y, z = position()
    sibling = (group + 1 - 2 * core, shard)
    x_peer = ((1 - x) * 2 + core, shard)
    y_peer = (group, 2 * z + 1 - y)
    z_of = [lax.rem(z + dz, 4) for dz in range(4)]
    y_of = [y, 1 - y]
    shard_peers = [(dz, dy) for dz in range(4) for dy in range(2) if dz + dy > 0]
    plane = [(dg, dy) for dg in range(4) for dy in range(2) if dg + dy > 0]
    plane_to = [(lax.rem(group + dg, 4), y_of[dy]) for dg, dy in plane]
    plane_from = [(lax.rem(group + 4 - dg, 4), y_of[dy]) for dg, dy in plane]
    outside = [(pg, 2 * z + py) for (pg, py), (dg, dy) in zip(plane_to, plane) if dg > 0]
    greet(outside + [(group, 2 * z_of[dz] + y_of[dy]) for dz, dy in shard_peers])

    def remote(src, dst, send, recv, device):
        return pltpu.make_async_remote_copy(
            src_ref=src, dst_ref=dst, send_sem=send, recv_sem=recv, device_id=device, device_id_type=MESH
        )

    def partial(factor, dst):
        if factor == 0:
            rows = hid[...]
        elif factor == 1:
            rows = ginp[...]
        elif factor == 7:
            rows = qry[...]
        else:
            rows = outg[factor - 2]
        at = 0
        for i in range(3):
            prod = lax.dot_general(
                rows[:, BLK * i:BLK * (i + 1)], rows[:, BLK * i:], (((0,), (0,)), ((), ())),
                preferred_element_type=jnp.float32,
            ).astype(jnp.bfloat16)
            for j in range(3 - i):
                dst[at * BLK:(at + 1) * BLK, :] = prod[:, BLK * j:BLK * (j + 1)]
                at += 1

    grad_copies = []
    for i, (dz, dy) in enumerate(shard_peers):
        grad_copies.append(remote(wgr.at[weight_of(core, y_of[dy], x)], gfull.at[pl.ds(shard * 96, 96)], gs.at[i],
                                  gr.at[i], (group, 2 * z_of[dz] + y_of[dy])))

        @pl.when(core + y_of[dy] > 0)
        def _(copy=grad_copies[-1]):
            copy.start()

    local = pltpu.make_async_copy(wgr.at[weight_of(core, y, x)], gfull.at[pl.ds(shard * 96, 96)], lsem)
    local.start()
    core_copies = [remote(sendb.at[j], rc.at[j], cs.at[j], cr.at[j], sibling) for j in range(4)]
    for owner in range(2):
        @pl.when(core != owner)
        def _():
            for j in range(4):
                partial(4 * owner + j, sendb.at[j])
                core_copies[j].start()

    for owner in range(2):
        @pl.when(core == owner)
        def _():
            for j in range(4):
                partial(4 * owner + j, keep.at[j])

    for j in range(4):
        core_copies[j].wait()

    def first_of(h, q):
        rows = pl.ds(h * HALF + q * SUB, SUB)
        into = pl.ds(q * SUB, SUB)
        if h == 0:
            return [remote(keep.at[2 * t + 1 - x, rows], r2.at[0, t, into], as_.at[h, q, t], ar.at[h, q, t], x_peer)
                    for t in range(2)]
        return [remote(keep.at[2 * (1 - y) + t, rows], r2.at[1, t, into], as_.at[h, q, t], ar.at[h, q, t], y_peer)
                for t in range(2)]

    passed = [2 * (1 - y) + x, 2 * y + 1 - x]
    other = [1 - y, 1 - x]
    same = [y, x]
    mine = 2 * y + x
    halves = [(h, q) for q in range(PARTS) for h in range(2)]
    first = {hq: first_of(*hq) for hq in halves}
    second = {(h, q): remote(keep.at[passed[h], pl.ds(h * HALF + q * SUB, SUB)], r3.at[h, pl.ds(q * SUB, SUB)],
                             bs.at[h, q], br.at[h, q], [y_peer, x_peer][h]) for h, q in halves}

    def own_rows(h, q):
        return h * HALF + q * SUB + z * ZROWS

    def scatter_of(h, q):
        return [remote(acc.at[pl.ds(h * HALF + q * SUB + z_of[dz] * ZROWS, ZROWS)], zr.at[h, q, dz - 1],
                       zs.at[h, q, dz - 1], zrs.at[h, q, dz - 1], (group, 2 * z_of[dz] + y)) for dz in range(1, 4)]

    def gather_of(h, q):
        rows = pl.ds(own_rows(h, q), ZROWS)
        return [remote(cov.at[rows], cov.at[rows], fs.at[h, q, dz - 1], fr.at[h, q, dz - 1],
                       (group, 2 * z_of[dz] + y)) for dz in range(1, 4)]

    scatter = {hq: scatter_of(*hq) for hq in halves}
    gather = {hq: gather_of(*hq) for hq in halves}

    def begin(q):
        for h in range(2):
            base = h * HALF + q * SUB
            for j in range(4):
                def store(at, value, j=j, base=base):
                    keep[j, pl.ds(base + at, STEP), :] = value

                add_rows(store, [lambda at, j=j, base=base: keep[j, pl.ds(base + at, STEP), :],
                                 lambda at, j=j, base=base: rc[j, pl.ds(base + at, STEP), :]], SUB)
            for copy in first[h, q]:
                copy.start()

    def pass_on(q):
        for h in range(2):
            base = h * HALF + q * SUB
            for copy in first[h, q]:
                copy.wait()

            def store(at, value, h=h, base=base):
                keep[passed[h], pl.ds(base + at, STEP), :] = value

            add_rows(store, [lambda at, h=h, base=base: keep[passed[h], pl.ds(base + at, STEP), :],
                             lambda at, h=h: r2[h, other[h], pl.ds(q * SUB + at, STEP), :]], SUB)
            second[h, q].start()

    def along_z(q):
        for h in range(2):
            base = h * HALF + q * SUB
            second[h, q].wait()

            def store(at, value, base=base):
                acc[pl.ds(base + at, STEP), :] = value

            add_rows(store, [lambda at, base=base: keep[mine, pl.ds(base + at, STEP), :],
                             lambda at, h=h: r2[h, same[h], pl.ds(q * SUB + at, STEP), :],
                             lambda at, h=h: r3[h, pl.ds(q * SUB + at, STEP), :]], SUB)
            for copy in scatter[h, q]:
                copy.start()

    def share(q):
        for h in range(2):
            base = own_rows(h, q)
            for copy in scatter[h, q]:
                copy.wait()

            def store(at, value, base=base):
                cov[pl.ds(base + at, STEP), :] = value

            loads = [lambda at, base=base: acc[pl.ds(base + at, STEP), :]]
            loads += [lambda at, h=h, d=d: zr[h, q, d, pl.ds(at, STEP), :] for d in range(3)]
            add_rows(store, loads, ZROWS)
            for copy in gather[h, q]:
                copy.start()

    begin(0)
    pass_on(0)
    begin(1)
    along_z(0)
    pass_on(1)
    share(0)
    along_z(1)
    share(1)
    for hq in halves:
        for copy in gather[hq]:
            copy.wait()

    trio = range(3)
    width = 3 * BLK
    sheet = [(lax.broadcasted_iota(jnp.int32, (BLK, width), 0) + BLK * i)
             == lax.broadcasted_iota(jnp.int32, (BLK, width), 1) for i in trio]
    rows_of = [pl.ds(BLK * i, BLK) for i in trio]

    def off_part(i, value):
        return jnp.where(sheet[i], 0.0, value)

    def diag_col(i, value):
        return jnp.sum(jnp.where(sheet[i], value, 0.0), axis=1, keepdims=True)

    def diag_row(i, value):
        return jnp.sum(jnp.where(sheet[i], value, 0.0), axis=0, keepdims=True)

    at = 0
    for i in trio:
        for j in range(i, 3):
            block = cov[at * BLK:(at + 1) * BLK, :].astype(jnp.float32)
            off_a[BLK * i:BLK * (i + 1), BLK * j:BLK * (j + 1)] = block
            if j > i:
                off_a[BLK * j:BLK * (j + 1), BLK * i:BLK * (i + 1)] = block.T
            at += 1
    col = []
    row, sums = jnp.zeros((1, width), jnp.float32), jnp.zeros((1, width), jnp.float32)
    for i in trio:
        value = off_a[rows_of[i], :]
        col.append(diag_col(i, value))
        row = row + diag_row(i, value)
        sums = sums + jnp.sum(jnp.abs(value), axis=0, keepdims=True)
    scale = width / jnp.sum(row, axis=1, keepdims=True)
    limit = jnp.max(sums, axis=1, keepdims=True) * scale + DAMPING
    shrink = scale / limit
    a_col = [part * shrink + DAMPING / limit for part in col]
    a_row = row * shrink + DAMPING / limit
    for i in trio:
        value = off_part(i, off_a[rows_of[i], :]) * shrink
        off_a[rows_of[i], :] = value
        nar_a[rows_of[i], :] = value.astype(jnp.bfloat16)

    def cross(left_col, left_off, left_nar, right_row, right_off, right_nar, i):
        value = jnp.dot(left_nar[rows_of[i], :], right_nar[...], preferred_element_type=jnp.float32)
        return value + left_col[i] * right_off[rows_of[i], :] + left_off[rows_of[i], :] * right_row

    b_col, b_row = [], a_row * a_row
    for i in trio:
        value = cross(a_col, off_a, nar_a, a_row, off_a, nar_a, i)
        b_col.append(a_col[i] * a_col[i] + diag_col(i, value))
        b_row = b_row + diag_row(i, value)
        value = off_part(i, value)
        off_b[rows_of[i], :] = value
        nar_b[rows_of[i], :] = value.astype(jnp.bfloat16)
    r_col, y_col = [], []
    y_row = 4.0 * a_row - 6.0 * b_row + 4.0 * a_row * b_row - b_row * b_row
    for i in trio:
        third = cross(a_col, off_a, nar_a, b_row, off_b, nar_b, i)
        fourth = cross(b_col, off_b, nar_b, b_row, off_b, nar_b, i)
        fa, fb = off_a[rows_of[i], :], off_b[rows_of[i], :]
        rest = 4.0 * fb - 6.0 * fa - third
        prod = 4.0 * fa - 6.0 * fb + 4.0 * third - fourth
        ac, bc = a_col[i], b_col[i]
        r_col.append(4.0 * bc - 6.0 * ac - ac * bc + diag_col(i, rest))
        y_col.append(4.0 * ac - 6.0 * bc + 4.0 * ac * bc - bc * bc + diag_col(i, prod))
        y_row = y_row + diag_row(i, prod)
        rest, prod = off_part(i, rest), off_part(i, prod)
        off_r[rows_of[i], :] = rest
        off_y[rows_of[i], :] = prod
        nar_r[rows_of[i], :] = rest.astype(jnp.bfloat16)
        nar_y[rows_of[i], :] = prod.astype(jnp.bfloat16)
    inverse_row = jnp.zeros((1, width), jnp.float32)
    for i in trio:
        value = cross(r_col, off_r, nar_r, y_row, off_y, nar_y, i)
        value = 2.0 * off_r[rows_of[i], :] - 4.0 * off_y[rows_of[i], :] - value
        diag = 8.0 + 2.0 * r_col[i] - 4.0 * y_col[i] - r_col[i] * y_col[i]
        inverse_row = inverse_row + diag_row(i, value + diag)
        nar_a[rows_of[i], :] = off_part(i, value / limit).astype(jnp.bfloat16)
    for f in range(8):
        @pl.when(4 * core + mine == f)
        def _(f=f):
            dall[f] = inverse_row / limit

    local.wait()
    for (dz, dy), copy in zip(shard_peers, grad_copies):
        @pl.when(core + y > 0)
        def _(copy=copy):
            copy.wait_recv()

        @pl.when(core + y_of[dy] > 0)
        def _(copy=copy):
            copy.wait_send()

    weight = weight_of(core, y, x)
    factor = 4 * core + mine
    diag_copies = [remote(dall.at[factor], dall.at[factor], ds_.at[i], dr.at[i], (pg, 2 * z + py))
                   for i, (pg, py) in enumerate(plane_to)]
    for copy in diag_copies:
        copy.start()
    left_copies = [remote(left.at[py], lout.at[weight], ls.at[i], lr.at[i], (pg, 2 * z + py))
                   for i, (pg, py) in enumerate(plane_to)]
    input_copies = [remote(nar_a.at[pl.ds(192 * pg, 192)], xout.at[x], ls.at[i], lr.at[i], (pg, 2 * z + py))
                    for i, (pg, py) in enumerate(plane_to)]

    @pl.when(core + y > 0)
    def _():
        for t in range(2):
            rows = nar_a[pl.ds(pl.multiple_of(z * 192 + t * 96, 16), 96), :]
            left[t] = jnp.dot(rows, gfull[...], preferred_element_type=jnp.float32).astype(jnp.bfloat16)
        for copy in left_copies:
            copy.start()
        own = pltpu.make_async_copy(left.at[y], lout.at[weight], lsem2)
        own.start()
        own.wait()
        for copy in left_copies:
            copy.wait_send()

    @pl.when(core + y == 0)
    def _():
        for copy in input_copies:
            copy.start()
        own = pltpu.make_async_copy(nar_a.at[pl.ds(192 * group, 192)], xout.at[x], lsem2)
        own.start()
        own.wait()
        for copy in input_copies:
            copy.wait_send()

    for i, (pg, py) in enumerate(plane_from):
        diag_copies[i].wait()

        @pl.when(lax.rem(pg, 2) + py > 0)
        def _(i=i):
            left_copies[i].wait_recv()

        @pl.when(lax.rem(pg, 2) + py == 0)
        def _(i=i):
            input_copies[i].wait_recv()


def fast_device(hidden, out_grads, global_inputs, query_grads, weight_grads, momentum):
    width = hidden.shape[1]
    group, shard, core, x, y, z = position()
    vmem = pl.BlockSpec(memory_space=pltpu.VMEM)
    dma = pltpu.SemaphoreType.DMA
    bf16, f32 = jnp.bfloat16, jnp.float32
    square, packed = (width, width), (2 * HALF, BLK)
    left_all, input_all, diag_all = pl.pallas_call(
        step_kernel,
        out_shape=(jax.ShapeDtypeStruct((6, 96, width), bf16), jax.ShapeDtypeStruct((2, 192, width), bf16),
                   jax.ShapeDtypeStruct((8, 1, width), f32)),
        in_specs=[vmem] * 5,
        out_specs=(vmem, vmem, vmem),
        scratch_shapes=[
            pltpu.VMEM((4,) + packed, bf16), pltpu.VMEM((4,) + packed, bf16), pltpu.VMEM((4,) + packed, bf16),
            pltpu.VMEM((2, 2, HALF, BLK), bf16), pltpu.VMEM((2, HALF, BLK), bf16), pltpu.VMEM(packed, bf16),
            pltpu.VMEM((2, PARTS, 3, ZROWS, BLK), bf16), pltpu.VMEM(packed, bf16), pltpu.VMEM(square, bf16),
        ] + [pltpu.VMEM(square, f32)] * 4 + [pltpu.VMEM(square, bf16)] * 4 + [
            pltpu.VMEM((2, 96, width), bf16),
            dma((4,)), dma((4,)), dma((2, PARTS, 2)), dma((2, PARTS, 2)), dma((2, PARTS)), dma((2, PARTS)),
            dma((2, PARTS, 3)), dma((2, PARTS, 3)), dma((2, PARTS, 3)), dma((2, PARTS, 3)), dma((7,)), dma((7,)),
            dma((7,)), dma((7,)), dma((7,)), dma((7,)), dma, dma, dma,
        ],
        compiler_params=pltpu.CompilerParams(collective_id=0, has_side_effects=True, vmem_limit_bytes=48 * 2**20),
    )(hidden, global_inputs, out_grads, query_grads, weight_grads)
    out_diag = lax.dynamic_slice_in_dim(diag_all[2:8, 0], shard * 96, 96, 1)
    left_side = out_diag[:, :, None] * weight_grads.astype(f32) + left_all.astype(f32)
    in_diag = lax.dynamic_slice_in_dim(diag_all[0:2, 0], group * 192, 192, 1)
    columns = lax.dynamic_slice_in_dim(left_side, group * 192, 192, 2)
    narrow = left_side.astype(bf16)

    def right(rows, which):
        return lax.dot_general(rows, input_all[which], (((rows.ndim - 1,), (1,)), ((), ())),
                               preferred_element_type=f32)

    step = jnp.concatenate([
        right(narrow[0:5], 0) + columns[0:5] * in_diag[0],
        (right(narrow[5], 1) + columns[5] * in_diag[1])[None],
    ], axis=0)
    return MOMENTUM * momentum + step


def solution(mesh):
    placed = (
        P(("group", "shard"), None),
        P(None, ("group", "shard"), None),
        P(("group", "shard"), None),
        P(("group", "shard"), None),
        P(None, "shard", None),
        P(None, "shard", "group"),
    )
    pairs = mesh.shape["group"] == 4 and mesh.shape["shard"] == 8
    return jax.shard_map(
        fast_device if pairs else on_device, mesh=mesh, in_specs=placed, out_specs=P(None, "shard", "group"), check_vma=False
    )
```

```python
import jax
import jax.numpy as jnp
from jax import lax
from jax.experimental import pallas as pl
from jax.experimental.pallas import tpu as pltpu
from jax.sharding import PartitionSpec as P

ITERS = 3


PRECISE = lax.Precision.HIGHEST
DAMPING = 0.1
MOMENTUM = 0.9


def broadcast(array, axis, root):
    mine = lax.axis_index(axis) == root
    return lax.psum(jnp.where(mine, array, jnp.zeros_like(array)), axis)


def outer_sum(matrix_rows):
    return lax.dot_general(
        matrix_rows, matrix_rows, (((0,), (0,)), ((), ())), preferred_element_type=jnp.float32
    )


def on_device(hidden, out_grads, global_inputs, query_grads, weight_grads, momentum):
    model_width = hidden.shape[1]
    group_size = lax.axis_size("group")
    shard_size = lax.axis_size("shard")
    per_group = 8 // group_size
    row_block = model_width // shard_size
    col_block = momentum.shape[2]
    shard_pos = lax.axis_index("shard")
    group_pos = lax.axis_index("group")
    devices = group_size * shard_size
    partials = [outer_sum(hidden), outer_sum(global_inputs)]
    partials = partials + [outer_sum(out_grads[member]) for member in range(5)]
    partials = partials + [outer_sum(query_grads)]
    stacked = jnp.stack([single.astype(jnp.bfloat16) for single in partials])
    summed = lax.psum_scatter(stacked, "group", scatter_dimension=0, tiled=True).astype(jnp.float32)
    factor_ids = group_pos * per_group + jnp.arange(per_group)
    is_global = (factor_ids == 1) | (factor_ids == 7)
    samp_total = float(hidden.shape[0] * devices)
    glob_total = float(global_inputs.shape[0] * devices)
    counted = jnp.where(is_global, glob_total, samp_total).astype(jnp.float32)
    factor_full = lax.psum(summed, "shard")
    covariance = factor_full / counted[:, None, None]
    mean_diag = jnp.trace(covariance, axis1=1, axis2=2) / model_width
    eye_full = jnp.eye(model_width, dtype=jnp.float32)
    matrix = covariance / mean_diag[:, None, None] + DAMPING * eye_full
    row_limit = jnp.max(jnp.sum(jnp.abs(matrix), axis=2), axis=1)
    approx = jnp.broadcast_to(eye_full, matrix.shape) / row_limit[:, None, None]
    for iteration in range(ITERS):
        product = jnp.einsum("kij,kjl->kil", matrix, approx, precision=PRECISE)
        approx = 2.0 * approx - jnp.einsum("kij,kjl->kil", approx, product, precision=PRECISE)
    own_rows = lax.dynamic_slice_in_dim(approx, shard_pos * row_block, row_block, 1)
    all_rows = lax.all_gather(own_rows, "group", axis=0, tiled=True)
    input_inv = jnp.stack(
        [broadcast(approx[factor % per_group], "group", factor // per_group) for factor in range(2)]
    )
    input_cols = lax.dynamic_slice_in_dim(input_inv, group_pos * col_block, col_block, 2)
    out_inverse = all_rows[2:8]
    initial = jnp.zeros(out_inverse.shape, jnp.float32)
    gathered = lax.all_gather(weight_grads, "shard", axis=1, tiled=True)
    columns = lax.slice_in_dim(out_inverse, 0, gathered.shape[1], axis=2)
    left_side = initial + jnp.einsum(
        "wrn,wnd->wrd", columns, gathered.astype(jnp.float32), precision=PRECISE
    )
    local_part = jnp.einsum("wrd,de->wre", left_side[0:5], input_cols[0], precision=PRECISE)
    global_part = jnp.dot(left_side[5], input_cols[1], precision=PRECISE)[None]
    return MOMENTUM * momentum + jnp.concatenate([local_part, global_part], axis=0)


MESH = pl.DeviceIdType.MESH
BLK = 256
HALF = 768
PARTS = 3
STEP = 32
FACTOR_AT = (0, 3, 2, 1, 4, 5, 6, 7)


def position():
    group, shard = lax.axis_index("group"), lax.axis_index("shard")
    core, x = lax.rem(group, 2), group // 2
    y, z = lax.rem(shard, 2), shard // 2
    return group, shard, core, x, y, z


def weight_of(core, y, x):
    return core * (2 + 2 * y + x) + (1 - core) * (1 - y)


def kind_of(core, y, x):
    return core + (x - y) * (x - y)


def greet(peers):
    barrier = pltpu.get_barrier_semaphore()
    for peer in peers:
        pl.semaphore_signal(barrier, inc=1, device_id=peer, device_id_type=MESH)
    pl.semaphore_wait(barrier, len(peers))


def add_rows(store, loads, rows):
    def step(i, carry):
        at = pl.multiple_of(i * STEP, STEP)
        total = loads[0](at).astype(jnp.float32)
        for load in loads[1:]:
            total = total + load(at).astype(jnp.float32)
        store(at, total.astype(jnp.bfloat16))
        return carry

    lax.fori_loop(0, rows // STEP, step, 0)


def step_kernel(hid, ginp, outg, qry, wgr, lout, xout, dall, hidv, ginpv, outgv, qryv, sendb, keep, rc, r2, r3, acc,
                zr1, zr2, cov, gfull, off_a, off_b, off_r, off_y, nar_a, nar_b, nar_r, nar_y, left,
                cs, cr, as_, ar, bs, br, zs, zrs, fs, fr, gs, gr, ls, lr, ds_, dr, is_, ir, rs, ins, lsem, lsem2):
    group, shard, core, x, y, z = position()
    sibling = (group + 1 - 2 * core, shard)
    x_peer = ((1 - x) * 2 + core, shard)
    y_peer = (group, 2 * z + 1 - y)
    z_of = [lax.rem(z + dz, 4) for dz in range(4)]
    y_of = [y, 1 - y]
    shard_peers = [(dz, dy) for dz in range(4) for dy in range(2) if dz + dy > 0]
    plane = [(dg, dy) for dg in range(4) for dy in range(2) if dg + dy > 0]
    plane_to = [(lax.rem(group + dg, 4), y_of[dy]) for dg, dy in plane]
    plane_from = [(lax.rem(group + 4 - dg, 4), y_of[dy]) for dg, dy in plane]
    outside = [(pg, 2 * z + py) for (pg, py), (dg, dy) in zip(plane_to, plane) if dg > 0]
    loads = [pltpu.make_async_copy(hid, hidv, ins.at[0]), pltpu.make_async_copy(ginp, ginpv, ins.at[1])]
    loads += [pltpu.make_async_copy(outg.at[i], outgv.at[i], ins.at[2 + i]) for i in range(5)]
    loads += [pltpu.make_async_copy(qry, qryv, ins.at[7])]
    for i in (4, 5, 6, 7, 0, 1, 2, 3):
        loads[i].start()
    greet(outside + [(group, 2 * z_of[dz] + y_of[dy]) for dz, dy in shard_peers])

    def remote(src, dst, send, recv, device):
        return pltpu.make_async_remote_copy(
            src_ref=src, dst_ref=dst, send_sem=send, recv_sem=recv, device_id=device, device_id_type=MESH
        )

    def partial(factor, dst):
        loads[factor].wait()
        if factor == 0:
            rows = hidv[...]
        elif factor == 1:
            rows = ginpv[...]
        elif factor == 7:
            rows = qryv[...]
        else:
            rows = outgv[factor - 2]
        at = 0
        for i in range(3):
            prod = lax.dot_general(
                rows[:, BLK * i:BLK * (i + 1)], rows[:, BLK * i:], (((0,), (0,)), ((), ())),
                preferred_element_type=jnp.float32,
            ).astype(jnp.bfloat16)
            for j in range(3 - i):
                dst[at * BLK:(at + 1) * BLK, :] = prod[:, BLK * j:BLK * (j + 1)]
                at += 1

    grad_copies = []
    for i, (dz, dy) in enumerate(shard_peers):
        grad_copies.append(remote(wgr.at[weight_of(core, y_of[dy], x)], gfull.at[pl.ds(shard * 96, 96)], gs.at[i],
                                  gr.at[i], (group, 2 * z_of[dz] + y_of[dy])))

        @pl.when(kind_of(core, y_of[dy], x) > 0)
        def _(copy=grad_copies[-1]):
            copy.start()

    local = pltpu.make_async_copy(wgr.at[weight_of(core, y, x)], gfull.at[pl.ds(shard * 96, 96)], lsem)
    local.start()
    core_copies = [[remote(sendb.at[j, pl.ds(512 * q, 512)], rc.at[j, pl.ds(512 * q, 512)], cs.at[j, q], cr.at[j, q],
                           sibling) for q in range(PARTS)] for j in range(4)]
    for owner in range(2):
        @pl.when(core != owner)
        def _():
            for j in range(4):
                partial(FACTOR_AT[4 * owner + j], sendb.at[j])
                core_copies[j][0].start()
            for q in range(1, PARTS):
                for j in range(4):
                    core_copies[j][q].start()

    for owner in range(2):
        @pl.when(core == owner)
        def _():
            for j in range(4):
                partial(FACTOR_AT[4 * owner + j], keep.at[j])

    passed = [2 * (1 - y) + x, 2 * y + 1 - x]
    other = [1 - y, 1 - x]
    same = [y, x]
    mine = 2 * y + x
    zh, zl = z // 2, lax.rem(z, 2)
    near = (group, 2 * (z + 1 - 2 * zl) + y)
    far = (group, 2 * (z + 2 - 4 * zh) + y)

    def first_of(h, q):
        rows = pl.ds(512 * q + BLK * h, BLK)
        if h == 0:
            return [remote(keep.at[2 * t + 1 - x, rows], r2.at[0, q, t], as_.at[h, q, t], ar.at[h, q, t], x_peer)
                    for t in range(2)]
        return [remote(keep.at[2 * (1 - y) + t, rows], r2.at[1, q, t], as_.at[h, q, t], ar.at[h, q, t], y_peer)
                for t in range(2)]

    halves = [(h, q) for q in range(PARTS) for h in range(2)]
    first = {hq: first_of(*hq) for hq in halves}
    second = {(h, q): remote(keep.at[passed[h], pl.ds(512 * q + BLK * h, BLK)], r3.at[h, q],
                             bs.at[h, q], br.at[h, q], [y_peer, x_peer][h]) for h, q in halves}

    def quarter(q):
        return 512 * q + 256 * zl + 128 * zh

    halve = [remote(acc.at[pl.ds(512 * q + 256 * (1 - zl), 256)], zr1.at[q], zs.at[0, q], zrs.at[0, q], near)
             for q in range(PARTS)]
    halve2 = [remote(acc.at[pl.ds(512 * q + 256 * zl + 128 * (1 - zh), 128)], zr2.at[q], zs.at[1, q], zrs.at[1, q],
                     far) for q in range(PARTS)]
    double = [remote(cov.at[pl.ds(quarter(q), 128)], cov.at[pl.ds(quarter(q), 128)], fs.at[0, q], fr.at[0, q], far)
              for q in range(PARTS)]
    double2 = [remote(cov.at[pl.ds(512 * q + 256 * zl, 256)], cov.at[pl.ds(512 * q + 256 * zl, 256)], fs.at[1, q],
                      fr.at[1, q], near) for q in range(PARTS)]

    def begin(q):
        base = 512 * q
        for j in range(4):
            core_copies[j][q].wait()

            def store(at, value, j=j):
                keep[j, pl.ds(base + at, STEP), :] = value

            add_rows(store, [lambda at, j=j: keep[j, pl.ds(base + at, STEP), :],
                             lambda at, j=j: rc[j, pl.ds(base + at, STEP), :]], 512)
        for t in range(2):
            for h in range(2):
                first[h, q][t].start()

    def pass_on(q):
        for h in range(2):
            base = 512 * q + BLK * h
            for copy in first[h, q]:
                copy.wait()

            def store(at, value, h=h, base=base):
                keep[passed[h], pl.ds(base + at, STEP), :] = value

            add_rows(store, [lambda at, h=h, base=base: keep[passed[h], pl.ds(base + at, STEP), :],
                             lambda at, h=h: r2[h, q, other[h], pl.ds(at, STEP), :]], BLK)
            second[h, q].start()

    def z_near(q):
        for h in range(2):
            base = 512 * q + BLK * h
            second[h, q].wait()

            def store(at, value, base=base):
                acc[pl.ds(base + at, STEP), :] = value

            add_rows(store, [lambda at, base=base: keep[mine, pl.ds(base + at, STEP), :],
                             lambda at, h=h: r2[h, q, same[h], pl.ds(at, STEP), :],
                             lambda at, h=h: r3[h, q, pl.ds(at, STEP), :]], BLK)
        halve[q].start()

    def z_far(q):
        base = 512 * q + 256 * zl
        halve[q].wait()

        def store(at, value):
            acc[pl.ds(base + at, STEP), :] = value

        add_rows(store, [lambda at: acc[pl.ds(base + at, STEP), :], lambda at: zr1[q, pl.ds(at, STEP), :]], 256)
        halve2[q].start()

    def back_far(q):
        base = quarter(q)
        halve2[q].wait()

        def store(at, value):
            cov[pl.ds(base + at, STEP), :] = value

        add_rows(store, [lambda at: acc[pl.ds(base + at, STEP), :], lambda at: zr2[q, pl.ds(at, STEP), :]], 128)
        double[q].start()

    def back_near(q):
        double[q].wait()
        double2[q].start()

    stages = [begin, pass_on, z_near, z_far, back_far, back_near]
    for tick in range(PARTS + len(stages) - 1):
        for depth in reversed(range(len(stages))):
            if 0 <= tick - depth < PARTS:
                stages[depth](tick - depth)
    for copy in double2:
        copy.wait()

    trio = range(3)
    width = 3 * BLK
    sheet = [(lax.broadcasted_iota(jnp.int32, (BLK, width), 0) + BLK * i)
             == lax.broadcasted_iota(jnp.int32, (BLK, width), 1) for i in trio]
    rows_of = [pl.ds(BLK * i, BLK) for i in trio]

    def off_part(i, value):
        return jnp.where(sheet[i], 0.0, value)

    def diag_col(i, value):
        return jnp.sum(jnp.where(sheet[i], value, 0.0), axis=1, keepdims=True)

    def diag_row(i, value):
        return jnp.sum(jnp.where(sheet[i], value, 0.0), axis=0, keepdims=True)

    at = 0
    for i in trio:
        for j in range(i, 3):
            block = cov[at * BLK:(at + 1) * BLK, :].astype(jnp.float32)
            off_a[BLK * i:BLK * (i + 1), BLK * j:BLK * (j + 1)] = block
            if j > i:
                off_a[BLK * j:BLK * (j + 1), BLK * i:BLK * (i + 1)] = block.T
            at += 1
    col = []
    row, sums = jnp.zeros((1, width), jnp.float32), jnp.zeros((1, width), jnp.float32)
    for i in trio:
        value = off_a[rows_of[i], :]
        col.append(diag_col(i, value))
        row = row + diag_row(i, value)
        sums = sums + jnp.sum(jnp.abs(value), axis=0, keepdims=True)
    scale = width / jnp.sum(row, axis=1, keepdims=True)
    limit = jnp.max(sums, axis=1, keepdims=True) * scale + DAMPING
    shrink = scale / limit
    a_col = [part * shrink + DAMPING / limit for part in col]
    a_row = row * shrink + DAMPING / limit
    for i in trio:
        value = off_part(i, off_a[rows_of[i], :]) * shrink
        off_a[rows_of[i], :] = value
        nar_a[rows_of[i], :] = value.astype(jnp.bfloat16)

    def cross(left_col, left_off, left_nar, right_row, right_off, right_nar, i):
        value = jnp.dot(left_nar[rows_of[i], :], right_nar[...], preferred_element_type=jnp.float32)
        return value + left_col[i] * right_off[rows_of[i], :] + left_off[rows_of[i], :] * right_row

    b_col, b_row = [], a_row * a_row
    for i in trio:
        value = cross(a_col, off_a, nar_a, a_row, off_a, nar_a, i)
        b_col.append(a_col[i] * a_col[i] + diag_col(i, value))
        b_row = b_row + diag_row(i, value)
        value = off_part(i, value)
        off_b[rows_of[i], :] = value
        nar_b[rows_of[i], :] = value.astype(jnp.bfloat16)
    r_col, y_col = [], []
    y_row = 4.0 * a_row - 6.0 * b_row + 4.0 * a_row * b_row - b_row * b_row
    for i in trio:
        third = cross(a_col, off_a, nar_a, b_row, off_b, nar_b, i)
        fourth = cross(b_col, off_b, nar_b, b_row, off_b, nar_b, i)
        fa, fb = off_a[rows_of[i], :], off_b[rows_of[i], :]
        rest = 4.0 * fb - 6.0 * fa - third
        prod = 4.0 * fa - 6.0 * fb + 4.0 * third - fourth
        ac, bc = a_col[i], b_col[i]
        r_col.append(4.0 * bc - 6.0 * ac - ac * bc + diag_col(i, rest))
        y_col.append(4.0 * ac - 6.0 * bc + 4.0 * ac * bc - bc * bc + diag_col(i, prod))
        y_row = y_row + diag_row(i, prod)
        rest, prod = off_part(i, rest), off_part(i, prod)
        off_r[rows_of[i], :] = rest
        off_y[rows_of[i], :] = prod
        nar_r[rows_of[i], :] = rest.astype(jnp.bfloat16)
        nar_y[rows_of[i], :] = prod.astype(jnp.bfloat16)
    inverse_row = jnp.zeros((1, width), jnp.float32)
    for i in trio:
        value = cross(r_col, off_r, nar_r, y_row, off_y, nar_y, i)
        value = 2.0 * off_r[rows_of[i], :] - 4.0 * off_y[rows_of[i], :] - value
        diag = 8.0 + 2.0 * r_col[i] - 4.0 * y_col[i] - r_col[i] * y_col[i]
        inverse_row = inverse_row + diag_row(i, value + diag)
        nar_a[rows_of[i], :] = off_part(i, value / limit).astype(jnp.bfloat16)
    for f in range(8):
        @pl.when(4 * core + mine == f)
        def _(f=f):
            dall[f] = inverse_row / limit

    local.wait()
    for (dz, dy), copy in zip(shard_peers, grad_copies):
        @pl.when(kind_of(core, y, x) > 0)
        def _(copy=copy):
            copy.wait_recv()

        @pl.when(kind_of(core, y_of[dy], x) > 0)
        def _(copy=copy):
            copy.wait_send()

    weight = weight_of(core, y, x)
    factor = 4 * core + mine
    diag_copies = [remote(dall.at[factor], dall.at[factor], ds_.at[i], dr.at[i], (pg, 2 * z + py))
                   for i, (pg, py) in enumerate(plane_to)]
    for copy in diag_copies:
        copy.start()
    left_copies = [remote(left.at[py], lout.at[weight], ls.at[i], lr.at[i], (pg, 2 * z + py))
                   for i, (pg, py) in enumerate(plane_to)]
    straight = [(i, pg, py) for i, (pg, py) in enumerate(plane_to)]
    input_copies = [remote(nar_a.at[pl.ds(192 * pg, 192)], xout.at[y], is_.at[i], ir.at[y], (pg, 2 * z + py))
                    for i, pg, py in straight]
    relay = remote(xout.at[y], xout.at[y], rs, ir.at[y], y_peer)

    @pl.when(kind_of(core, y, x) > 0)
    def _():
        for t in range(2):
            rows = nar_a[pl.ds(pl.multiple_of(z * 192 + t * 96, 16), 96), :]
            left[t] = jnp.dot(rows, gfull[...], preferred_element_type=jnp.float32).astype(jnp.bfloat16)
        for copy in left_copies:
            copy.start()
        own = pltpu.make_async_copy(left.at[y], lout.at[weight], lsem2)
        own.start()
        own.wait()

    def to_straight(act):
        for copy, (i, pg, py) in zip(input_copies, straight):
            @pl.when((pg // 2 - x) * (py - y) == 0)
            def _(copy=copy):
                act(copy)

    @pl.when(kind_of(core, y, x) == 0)
    def _():
        to_straight(lambda copy: copy.start())
        own = pltpu.make_async_copy(nar_a.at[pl.ds(192 * group, 192)], xout.at[y], lsem2)
        own.start()
        own.wait()

    def arrived(which):
        remote(xout.at[which], xout.at[which], rs, ir.at[which], y_peer).wait_recv()

    @pl.when((x - y) * (x - y) > 0)
    def _():
        arrived(y)
        relay.start()
        arrived(1 - y)
        relay.wait_send()

    @pl.when((x - y) * (x - y) == 0)
    def _():
        arrived(1 - y)

        @pl.when(core > 0)
        def _():
            arrived(y)

    @pl.when(kind_of(core, y, x) > 0)
    def _():
        for copy in left_copies:
            copy.wait_send()

    @pl.when(kind_of(core, y, x) == 0)
    def _():
        to_straight(lambda copy: copy.wait_send())

    for i, (pg, py) in enumerate(plane_from):
        diag_copies[i].wait()

        @pl.when(kind_of(lax.rem(pg, 2), py, pg // 2) > 0)
        def _(i=i):
            left_copies[i].wait_recv()


def fast_device(hidden, out_grads, global_inputs, query_grads, weight_grads, momentum):
    width = hidden.shape[1]
    group, shard, core, x, y, z = position()
    vmem = pl.BlockSpec(memory_space=pltpu.VMEM)
    dma = pltpu.SemaphoreType.DMA
    bf16, f32 = jnp.bfloat16, jnp.float32
    square, packed = (width, width), (2 * HALF, BLK)
    left_all, input_all, diag_all = pl.pallas_call(
        step_kernel,
        out_shape=(jax.ShapeDtypeStruct((6, 96, width), bf16), jax.ShapeDtypeStruct((2, 192, width), bf16),
                   jax.ShapeDtypeStruct((8, 1, width), f32)),
        in_specs=[pl.BlockSpec(memory_space=pltpu.HBM)] * 5,
        out_specs=(vmem, vmem, vmem),
        scratch_shapes=[
            pltpu.VMEM(hidden.shape, bf16), pltpu.VMEM(global_inputs.shape, bf16),
            pltpu.VMEM(out_grads.shape, bf16), pltpu.VMEM(query_grads.shape, bf16),
            pltpu.VMEM((4,) + packed, bf16), pltpu.VMEM((4,) + packed, bf16), pltpu.VMEM((4,) + packed, bf16),
            pltpu.VMEM((2, PARTS, 2, BLK, BLK), bf16), pltpu.VMEM((2, PARTS, BLK, BLK), bf16),
            pltpu.VMEM(packed, bf16), pltpu.VMEM((PARTS, 256, BLK), bf16), pltpu.VMEM((PARTS, 128, BLK), bf16),
            pltpu.VMEM(packed, bf16), pltpu.VMEM(square, bf16),
        ] + [pltpu.VMEM(square, f32)] * 4 + [pltpu.VMEM(square, bf16)] * 4 + [
            pltpu.VMEM((2, 96, width), bf16),
            dma((4, PARTS)), dma((4, PARTS)), dma((2, PARTS, 2)), dma((2, PARTS, 2)), dma((2, PARTS)),
            dma((2, PARTS)), dma((2, PARTS)), dma((2, PARTS)), dma((2, PARTS)), dma((2, PARTS)), dma((7,)), dma((7,)),
            dma((7,)), dma((7,)), dma((7,)), dma((7,)), dma((7,)), dma((2,)), dma, dma((8,)), dma, dma,
        ],
        compiler_params=pltpu.CompilerParams(collective_id=0, has_side_effects=True, vmem_limit_bytes=48 * 2**20),
    )(hidden, global_inputs, out_grads, query_grads, weight_grads)
    out_diag = lax.dynamic_slice_in_dim(jnp.stack([diag_all[i, 0] for i in (2, 1, 4, 5, 6, 7)]), shard * 96, 96, 1)
    left_side = out_diag[:, :, None] * weight_grads.astype(f32) + left_all.astype(f32)
    in_diag = lax.dynamic_slice_in_dim(jnp.stack([diag_all[i, 0] for i in (0, 3)]), group * 192, 192, 1)
    columns = lax.dynamic_slice_in_dim(left_side, group * 192, 192, 2)
    narrow = left_side.astype(bf16)

    def right(rows, which):
        return lax.dot_general(rows, input_all[which], (((rows.ndim - 1,), (1,)), ((), ())),
                               preferred_element_type=f32)

    step = jnp.concatenate([
        right(narrow[0:5], 0) + columns[0:5] * in_diag[0],
        (right(narrow[5], 1) + columns[5] * in_diag[1])[None],
    ], axis=0)
    return MOMENTUM * momentum + step


def solution(mesh):
    placed = (
        P(("group", "shard"), None),
        P(None, ("group", "shard"), None),
        P(("group", "shard"), None),
        P(("group", "shard"), None),
        P(None, "shard", None),
        P(None, "shard", "group"),
    )
    pairs = mesh.shape["group"] == 4 and mesh.shape["shard"] == 8
    return jax.shard_map(
        fast_device if pairs else on_device, mesh=mesh, in_specs=placed, out_specs=P(None, "shard", "group"), check_vma=False
    )
```

```python
import jax
import jax.numpy as jnp
from jax import lax
from jax.experimental import pallas as pl
from jax.experimental.pallas import tpu as pltpu
from jax.sharding import PartitionSpec as P

ITERS = 3


PRECISE = lax.Precision.HIGHEST
DAMPING = 0.1
MOMENTUM = 0.9


def broadcast(array, axis, root):
    mine = lax.axis_index(axis) == root
    return lax.psum(jnp.where(mine, array, jnp.zeros_like(array)), axis)


def outer_sum(matrix_rows):
    return lax.dot_general(
        matrix_rows, matrix_rows, (((0,), (0,)), ((), ())), preferred_element_type=jnp.float32
    )


def on_device(hidden, out_grads, global_inputs, query_grads, weight_grads, momentum):
    model_width = hidden.shape[1]
    group_size = lax.axis_size("group")
    shard_size = lax.axis_size("shard")
    per_group = 8 // group_size
    row_block = model_width // shard_size
    col_block = momentum.shape[2]
    shard_pos = lax.axis_index("shard")
    group_pos = lax.axis_index("group")
    devices = group_size * shard_size
    partials = [outer_sum(hidden), outer_sum(global_inputs)]
    partials = partials + [outer_sum(out_grads[member]) for member in range(5)]
    partials = partials + [outer_sum(query_grads)]
    stacked = jnp.stack([single.astype(jnp.bfloat16) for single in partials])
    summed = lax.psum_scatter(stacked, "group", scatter_dimension=0, tiled=True).astype(jnp.float32)
    factor_ids = group_pos * per_group + jnp.arange(per_group)
    is_global = (factor_ids == 1) | (factor_ids == 7)
    samp_total = float(hidden.shape[0] * devices)
    glob_total = float(global_inputs.shape[0] * devices)
    counted = jnp.where(is_global, glob_total, samp_total).astype(jnp.float32)
    factor_full = lax.psum(summed, "shard")
    covariance = factor_full / counted[:, None, None]
    mean_diag = jnp.trace(covariance, axis1=1, axis2=2) / model_width
    eye_full = jnp.eye(model_width, dtype=jnp.float32)
    matrix = covariance / mean_diag[:, None, None] + DAMPING * eye_full
    row_limit = jnp.max(jnp.sum(jnp.abs(matrix), axis=2), axis=1)
    approx = jnp.broadcast_to(eye_full, matrix.shape) / row_limit[:, None, None]
    for iteration in range(ITERS):
        product = jnp.einsum("kij,kjl->kil", matrix, approx, precision=PRECISE)
        approx = 2.0 * approx - jnp.einsum("kij,kjl->kil", approx, product, precision=PRECISE)
    own_rows = lax.dynamic_slice_in_dim(approx, shard_pos * row_block, row_block, 1)
    all_rows = lax.all_gather(own_rows, "group", axis=0, tiled=True)
    input_inv = jnp.stack(
        [broadcast(approx[factor % per_group], "group", factor // per_group) for factor in range(2)]
    )
    input_cols = lax.dynamic_slice_in_dim(input_inv, group_pos * col_block, col_block, 2)
    out_inverse = all_rows[2:8]
    initial = jnp.zeros(out_inverse.shape, jnp.float32)
    gathered = lax.all_gather(weight_grads, "shard", axis=1, tiled=True)
    columns = lax.slice_in_dim(out_inverse, 0, gathered.shape[1], axis=2)
    left_side = initial + jnp.einsum(
        "wrn,wnd->wrd", columns, gathered.astype(jnp.float32), precision=PRECISE
    )
    local_part = jnp.einsum("wrd,de->wre", left_side[0:5], input_cols[0], precision=PRECISE)
    global_part = jnp.dot(left_side[5], input_cols[1], precision=PRECISE)[None]
    return MOMENTUM * momentum + jnp.concatenate([local_part, global_part], axis=0)


MESH = pl.DeviceIdType.MESH
BLK = 256
HALF = 768
PARTS = 3
STEP = 32
FACTOR_AT = (0, 3, 2, 1, 4, 5, 6, 7)


def position():
    group, shard = lax.axis_index("group"), lax.axis_index("shard")
    core, x = lax.rem(group, 2), group // 2
    y, z = lax.rem(shard, 2), shard // 2
    return group, shard, core, x, y, z


def weight_of(core, y, x):
    return core * (2 + 2 * y + x) + (1 - core) * (1 - y)


def kind_of(core, y, x):
    return core + (x - y) * (x - y)


def greet(peers):
    barrier = pltpu.get_barrier_semaphore()
    for peer in peers:
        pl.semaphore_signal(barrier, inc=1, device_id=peer, device_id_type=MESH)
    pl.semaphore_wait(barrier, len(peers))


def add_rows(store, loads, rows):
    def step(i, carry):
        at = pl.multiple_of(i * STEP, STEP)
        total = loads[0](at).astype(jnp.float32)
        for load in loads[1:]:
            total = total + load(at).astype(jnp.float32)
        store(at, total.astype(jnp.bfloat16))
        return carry

    lax.fori_loop(0, rows // STEP, step, 0)


def step_kernel(hid, ginp, outg, qry, wgr, lout, xout, dall, hidv, ginpv, outgv, qryv, sendb, keep, rc, r2, r3, acc,
                zr1, zr2, cov, gfull, off_a, off_b, off_r, off_y, nar_a, nar_b, nar_r, nar_y, left,
                cs, cr, as_, ar, bs, br, zs, zrs, fs, fr, gs, gr, ls, lr, ds_, dr, is_, ir, rs, ins, lsem, lsem2):
    group, shard, core, x, y, z = position()
    sibling = (group + 1 - 2 * core, shard)
    x_peer = ((1 - x) * 2 + core, shard)
    y_peer = (group, 2 * z + 1 - y)
    z_of = [lax.rem(z + dz, 4) for dz in range(4)]
    y_of = [y, 1 - y]
    shard_peers = [(dz, dy) for dz in range(4) for dy in range(2) if dz + dy > 0]
    plane = [(dg, dy) for dg in range(4) for dy in range(2) if dg + dy > 0]
    plane_to = [(lax.rem(group + dg, 4), y_of[dy]) for dg, dy in plane]
    plane_from = [(lax.rem(group + 4 - dg, 4), y_of[dy]) for dg, dy in plane]
    outside = [(pg, 2 * z + py) for (pg, py), (dg, dy) in zip(plane_to, plane) if dg > 0]
    loads = [pltpu.make_async_copy(hid, hidv, ins.at[0]), pltpu.make_async_copy(ginp, ginpv, ins.at[1])]
    loads += [pltpu.make_async_copy(outg.at[i], outgv.at[i], ins.at[2 + i]) for i in range(5)]
    loads += [pltpu.make_async_copy(qry, qryv, ins.at[7])]
    for i in (4, 5, 6, 7, 0, 1, 2, 3):
        loads[i].start()
    greet(outside + [(group, 2 * z_of[dz] + y_of[dy]) for dz, dy in shard_peers])

    def remote(src, dst, send, recv, device):
        return pltpu.make_async_remote_copy(
            src_ref=src, dst_ref=dst, send_sem=send, recv_sem=recv, device_id=device, device_id_type=MESH
        )

    def partial(factor, dst):
        loads[factor].wait()
        if factor == 0:
            rows = hidv[...]
        elif factor == 1:
            rows = ginpv[...]
        elif factor == 7:
            rows = qryv[...]
        else:
            rows = outgv[factor - 2]
        at = 0
        for i in range(3):
            prod = lax.dot_general(
                rows[:, BLK * i:BLK * (i + 1)], rows[:, BLK * i:], (((0,), (0,)), ((), ())),
                preferred_element_type=jnp.float32,
            ).astype(jnp.bfloat16)
            for j in range(3 - i):
                dst[at * BLK:(at + 1) * BLK, :] = prod[:, BLK * j:BLK * (j + 1)]
                at += 1

    grad_copies = []
    for i, (dz, dy) in enumerate(shard_peers):
        grad_copies.append(remote(wgr.at[weight_of(core, y_of[dy], x)], gfull.at[pl.ds(shard * 96, 96)], gs.at[i],
                                  gr.at[i], (group, 2 * z_of[dz] + y_of[dy])))

        @pl.when(kind_of(core, y_of[dy], x) > 0)
        def _(copy=grad_copies[-1]):
            copy.start()

    local = pltpu.make_async_copy(wgr.at[weight_of(core, y, x)], gfull.at[pl.ds(shard * 96, 96)], lsem)
    local.start()
    core_copies = [[remote(sendb.at[j, pl.ds(512 * q, 512)], rc.at[j, pl.ds(512 * q, 512)], cs.at[j, q], cr.at[j, q],
                           sibling) for q in range(PARTS)] for j in range(4)]
    for owner in range(2):
        @pl.when(core != owner)
        def _():
            for j in range(4):
                partial(FACTOR_AT[4 * owner + j], sendb.at[j])
                core_copies[j][0].start()
            for q in range(1, PARTS):
                for j in range(4):
                    core_copies[j][q].start()

    for owner in range(2):
        @pl.when(core == owner)
        def _():
            for j in range(4):
                partial(FACTOR_AT[4 * owner + j], keep.at[j])

    passed = [2 * (1 - y) + x, 2 * y + 1 - x]
    other = [1 - y, 1 - x]
    same = [y, x]
    mine = 2 * y + x
    zh, zl = z // 2, lax.rem(z, 2)
    near = (group, 2 * (z + 1 - 2 * zl) + y)
    far = (group, 2 * (z + 2 - 4 * zh) + y)

    def first_of(h, q):
        rows = pl.ds(512 * q + BLK * h, BLK)
        if h == 0:
            return [remote(keep.at[2 * t + 1 - x, rows], r2.at[0, q, t], as_.at[h, q, t], ar.at[h, q, t], x_peer)
                    for t in range(2)]
        return [remote(keep.at[2 * (1 - y) + t, rows], r2.at[1, q, t], as_.at[h, q, t], ar.at[h, q, t], y_peer)
                for t in range(2)]

    halves = [(h, q) for q in range(PARTS) for h in range(2)]
    first = {hq: first_of(*hq) for hq in halves}
    second = {(h, q): remote(keep.at[passed[h], pl.ds(512 * q + BLK * h, BLK)], r3.at[h, q],
                             bs.at[h, q], br.at[h, q], [y_peer, x_peer][h]) for h, q in halves}

    def quarter(q):
        return 512 * q + 256 * zl + 128 * zh

    halve = [remote(acc.at[pl.ds(512 * q + 256 * (1 - zl), 256)], zr1.at[q], zs.at[0, q], zrs.at[0, q], near)
             for q in range(PARTS)]
    halve2 = [remote(acc.at[pl.ds(512 * q + 256 * zl + 128 * (1 - zh), 128)], zr2.at[q], zs.at[1, q], zrs.at[1, q],
                     far) for q in range(PARTS)]
    double = [remote(cov.at[pl.ds(quarter(q), 128)], cov.at[pl.ds(quarter(q), 128)], fs.at[0, q], fr.at[0, q], far)
              for q in range(PARTS)]
    double2 = [remote(cov.at[pl.ds(512 * q + 256 * zl, 256)], cov.at[pl.ds(512 * q + 256 * zl, 256)], fs.at[1, q],
                      fr.at[1, q], near) for q in range(PARTS)]

    def begin(q):
        base = 512 * q
        for j in range(4):
            core_copies[j][q].wait()

            def store(at, value, j=j):
                keep[j, pl.ds(base + at, STEP), :] = value

            add_rows(store, [lambda at, j=j: keep[j, pl.ds(base + at, STEP), :],
                             lambda at, j=j: rc[j, pl.ds(base + at, STEP), :]], 512)
        for t in range(2):
            for h in range(2):
                first[h, q][t].start()

    def pass_on(q):
        for h in range(2):
            base = 512 * q + BLK * h
            for copy in first[h, q]:
                copy.wait()

            def store(at, value, h=h, base=base):
                keep[passed[h], pl.ds(base + at, STEP), :] = value

            add_rows(store, [lambda at, h=h, base=base: keep[passed[h], pl.ds(base + at, STEP), :],
                             lambda at, h=h: r2[h, q, other[h], pl.ds(at, STEP), :]], BLK)
            second[h, q].start()

    def z_near(q):
        for h in range(2):
            base = 512 * q + BLK * h
            second[h, q].wait()

            def store(at, value, base=base):
                acc[pl.ds(base + at, STEP), :] = value

            add_rows(store, [lambda at, base=base: keep[mine, pl.ds(base + at, STEP), :],
                             lambda at, h=h: r2[h, q, same[h], pl.ds(at, STEP), :],
                             lambda at, h=h: r3[h, q, pl.ds(at, STEP), :]], BLK)
        halve[q].start()

    def z_far(q):
        base = 512 * q + 256 * zl
        halve[q].wait()

        def store(at, value):
            acc[pl.ds(base + at, STEP), :] = value

        add_rows(store, [lambda at: acc[pl.ds(base + at, STEP), :], lambda at: zr1[q, pl.ds(at, STEP), :]], 256)
        halve2[q].start()

    def back_far(q):
        base = quarter(q)
        halve2[q].wait()

        def store(at, value):
            cov[pl.ds(base + at, STEP), :] = value

        add_rows(store, [lambda at: acc[pl.ds(base + at, STEP), :], lambda at: zr2[q, pl.ds(at, STEP), :]], 128)
        double[q].start()

    def back_near(q):
        double[q].wait()
        double2[q].start()

    stages = [begin, pass_on, z_near, z_far, back_far, back_near]
    for tick in range(PARTS + len(stages) - 1):
        for depth in range(len(stages)):
            if 0 <= tick - depth < PARTS:
                stages[depth](tick - depth)
    for copy in double2:
        copy.wait()

    trio = range(3)
    width = 3 * BLK
    sheet = [(lax.broadcasted_iota(jnp.int32, (BLK, width), 0) + BLK * i)
             == lax.broadcasted_iota(jnp.int32, (BLK, width), 1) for i in trio]
    rows_of = [pl.ds(BLK * i, BLK) for i in trio]

    def off_part(i, value):
        return jnp.where(sheet[i], 0.0, value)

    def diag_col(i, value):
        return jnp.sum(jnp.where(sheet[i], value, 0.0), axis=1, keepdims=True)

    def diag_row(i, value):
        return jnp.sum(jnp.where(sheet[i], value, 0.0), axis=0, keepdims=True)

    at = 0
    for i in trio:
        for j in range(i, 3):
            block = cov[at * BLK:(at + 1) * BLK, :].astype(jnp.float32)
            off_a[BLK * i:BLK * (i + 1), BLK * j:BLK * (j + 1)] = block
            if j > i:
                off_a[BLK * j:BLK * (j + 1), BLK * i:BLK * (i + 1)] = block.T
            at += 1
    col = []
    row, sums = jnp.zeros((1, width), jnp.float32), jnp.zeros((1, width), jnp.float32)
    for i in trio:
        value = off_a[rows_of[i], :]
        col.append(diag_col(i, value))
        row = row + diag_row(i, value)
        sums = sums + jnp.sum(jnp.abs(value), axis=0, keepdims=True)
    scale = width / jnp.sum(row, axis=1, keepdims=True)
    limit = jnp.max(sums, axis=1, keepdims=True) * scale + DAMPING
    shrink = scale / limit
    a_col = [part * shrink + DAMPING / limit for part in col]
    a_row = row * shrink + DAMPING / limit
    for i in trio:
        value = off_part(i, off_a[rows_of[i], :]) * shrink
        off_a[rows_of[i], :] = value
        nar_a[rows_of[i], :] = value.astype(jnp.bfloat16)

    def cross(left_col, left_off, left_nar, right_row, right_off, right_nar, i):
        value = jnp.dot(left_nar[rows_of[i], :], right_nar[...], preferred_element_type=jnp.float32)
        return value + left_col[i] * right_off[rows_of[i], :] + left_off[rows_of[i], :] * right_row

    b_col, b_row = [], a_row * a_row
    for i in trio:
        value = cross(a_col, off_a, nar_a, a_row, off_a, nar_a, i)
        b_col.append(a_col[i] * a_col[i] + diag_col(i, value))
        b_row = b_row + diag_row(i, value)
        value = off_part(i, value)
        off_b[rows_of[i], :] = value
        nar_b[rows_of[i], :] = value.astype(jnp.bfloat16)
    r_col, y_col = [], []
    y_row = 4.0 * a_row - 6.0 * b_row + 4.0 * a_row * b_row - b_row * b_row
    for i in trio:
        third = cross(a_col, off_a, nar_a, b_row, off_b, nar_b, i)
        fourth = cross(b_col, off_b, nar_b, b_row, off_b, nar_b, i)
        fa, fb = off_a[rows_of[i], :], off_b[rows_of[i], :]
        rest = 4.0 * fb - 6.0 * fa - third
        prod = 4.0 * fa - 6.0 * fb + 4.0 * third - fourth
        ac, bc = a_col[i], b_col[i]
        r_col.append(4.0 * bc - 6.0 * ac - ac * bc + diag_col(i, rest))
        y_col.append(4.0 * ac - 6.0 * bc + 4.0 * ac * bc - bc * bc + diag_col(i, prod))
        y_row = y_row + diag_row(i, prod)
        rest, prod = off_part(i, rest), off_part(i, prod)
        off_r[rows_of[i], :] = rest
        off_y[rows_of[i], :] = prod
        nar_r[rows_of[i], :] = rest.astype(jnp.bfloat16)
        nar_y[rows_of[i], :] = prod.astype(jnp.bfloat16)
    inverse_row = jnp.zeros((1, width), jnp.float32)
    for i in trio:
        value = cross(r_col, off_r, nar_r, y_row, off_y, nar_y, i)
        value = 2.0 * off_r[rows_of[i], :] - 4.0 * off_y[rows_of[i], :] - value
        diag = 8.0 + 2.0 * r_col[i] - 4.0 * y_col[i] - r_col[i] * y_col[i]
        inverse_row = inverse_row + diag_row(i, value + diag)
        nar_a[rows_of[i], :] = off_part(i, value / limit).astype(jnp.bfloat16)
    for f in range(8):
        @pl.when(4 * core + mine == f)
        def _(f=f):
            dall[f] = inverse_row / limit

    local.wait()
    for (dz, dy), copy in zip(shard_peers, grad_copies):
        @pl.when(kind_of(core, y, x) > 0)
        def _(copy=copy):
            copy.wait_recv()

        @pl.when(kind_of(core, y_of[dy], x) > 0)
        def _(copy=copy):
            copy.wait_send()

    weight = weight_of(core, y, x)
    factor = 4 * core + mine
    diag_copies = [remote(dall.at[factor], dall.at[factor], ds_.at[i], dr.at[i], (pg, 2 * z + py))
                   for i, (pg, py) in enumerate(plane_to)]
    for copy in diag_copies:
        copy.start()
    left_copies = [remote(left.at[py], lout.at[weight], ls.at[i], lr.at[i], (pg, 2 * z + py))
                   for i, (pg, py) in enumerate(plane_to)]
    straight = [(i, pg, py) for i, (pg, py) in enumerate(plane_to)]
    input_copies = [remote(nar_a.at[pl.ds(192 * pg, 192)], xout.at[y], is_.at[i], ir.at[y], (pg, 2 * z + py))
                    for i, pg, py in straight]
    relay = remote(xout.at[y], xout.at[y], rs, ir.at[y], y_peer)

    @pl.when(kind_of(core, y, x) > 0)
    def _():
        for t in range(2):
            rows = nar_a[pl.ds(pl.multiple_of(z * 192 + t * 96, 16), 96), :]
            left[t] = jnp.dot(rows, gfull[...], preferred_element_type=jnp.float32).astype(jnp.bfloat16)
        for copy in left_copies:
            copy.start()
        own = pltpu.make_async_copy(left.at[y], lout.at[weight], lsem2)
        own.start()
        own.wait()

    def to_straight(act):
        for copy, (i, pg, py) in zip(input_copies, straight):
            @pl.when((pg // 2 - x) * (py - y) == 0)
            def _(copy=copy):
                act(copy)

    @pl.when(kind_of(core, y, x) == 0)
    def _():
        to_straight(lambda copy: copy.start())
        own = pltpu.make_async_copy(nar_a.at[pl.ds(192 * group, 192)], xout.at[y], lsem2)
        own.start()
        own.wait()

    def arrived(which):
        remote(xout.at[which], xout.at[which], rs, ir.at[which], y_peer).wait_recv()

    @pl.when((x - y) * (x - y) > 0)
    def _():
        arrived(y)
        relay.start()
        arrived(1 - y)
        relay.wait_send()

    @pl.when((x - y) * (x - y) == 0)
    def _():
        arrived(1 - y)

        @pl.when(core > 0)
        def _():
            arrived(y)

    @pl.when(kind_of(core, y, x) > 0)
    def _():
        for copy in left_copies:
            copy.wait_send()

    @pl.when(kind_of(core, y, x) == 0)
    def _():
        to_straight(lambda copy: copy.wait_send())

    for i, (pg, py) in enumerate(plane_from):
        diag_copies[i].wait()

        @pl.when(kind_of(lax.rem(pg, 2), py, pg // 2) > 0)
        def _(i=i):
            left_copies[i].wait_recv()


def fast_device(hidden, out_grads, global_inputs, query_grads, weight_grads, momentum):
    width = hidden.shape[1]
    group, shard, core, x, y, z = position()
    vmem = pl.BlockSpec(memory_space=pltpu.VMEM)
    dma = pltpu.SemaphoreType.DMA
    bf16, f32 = jnp.bfloat16, jnp.float32
    square, packed = (width, width), (2 * HALF, BLK)
    left_all, input_all, diag_all = pl.pallas_call(
        step_kernel,
        out_shape=(jax.ShapeDtypeStruct((6, 96, width), bf16), jax.ShapeDtypeStruct((2, 192, width), bf16),
                   jax.ShapeDtypeStruct((8, 1, width), f32)),
        in_specs=[pl.BlockSpec(memory_space=pltpu.HBM)] * 5,
        out_specs=(vmem, vmem, vmem),
        scratch_shapes=[
            pltpu.VMEM(hidden.shape, bf16), pltpu.VMEM(global_inputs.shape, bf16),
            pltpu.VMEM(out_grads.shape, bf16), pltpu.VMEM(query_grads.shape, bf16),
            pltpu.VMEM((4,) + packed, bf16), pltpu.VMEM((4,) + packed, bf16), pltpu.VMEM((4,) + packed, bf16),
            pltpu.VMEM((2, PARTS, 2, BLK, BLK), bf16), pltpu.VMEM((2, PARTS, BLK, BLK), bf16),
            pltpu.VMEM(packed, bf16), pltpu.VMEM((PARTS, 256, BLK), bf16), pltpu.VMEM((PARTS, 128, BLK), bf16),
            pltpu.VMEM(packed, bf16), pltpu.VMEM(square, bf16),
        ] + [pltpu.VMEM(square, f32)] * 4 + [pltpu.VMEM(square, bf16)] * 4 + [
            pltpu.VMEM((2, 96, width), bf16),
            dma((4, PARTS)), dma((4, PARTS)), dma((2, PARTS, 2)), dma((2, PARTS, 2)), dma((2, PARTS)),
            dma((2, PARTS)), dma((2, PARTS)), dma((2, PARTS)), dma((2, PARTS)), dma((2, PARTS)), dma((7,)), dma((7,)),
            dma((7,)), dma((7,)), dma((7,)), dma((7,)), dma((7,)), dma((2,)), dma, dma((8,)), dma, dma,
        ],
        compiler_params=pltpu.CompilerParams(collective_id=0, has_side_effects=True, vmem_limit_bytes=48 * 2**20),
    )(hidden, global_inputs, out_grads, query_grads, weight_grads)
    out_diag = lax.dynamic_slice_in_dim(jnp.stack([diag_all[i, 0] for i in (2, 1, 4, 5, 6, 7)]), shard * 96, 96, 1)
    left_side = out_diag[:, :, None] * weight_grads.astype(f32) + left_all.astype(f32)
    in_diag = lax.dynamic_slice_in_dim(jnp.stack([diag_all[i, 0] for i in (0, 3)]), group * 192, 192, 1)
    columns = lax.dynamic_slice_in_dim(left_side, group * 192, 192, 2)
    narrow = left_side.astype(bf16)

    def right(rows, which):
        return lax.dot_general(rows, input_all[which], (((rows.ndim - 1,), (1,)), ((), ())),
                               preferred_element_type=f32)

    step = jnp.concatenate([
        right(narrow[0:5], 0) + columns[0:5] * in_diag[0],
        (right(narrow[5], 1) + columns[5] * in_diag[1])[None],
    ], axis=0)
    return MOMENTUM * momentum + step


def solution(mesh):
    placed = (
        P(("group", "shard"), None),
        P(None, ("group", "shard"), None),
        P(("group", "shard"), None),
        P(("group", "shard"), None),
        P(None, "shard", None),
        P(None, "shard", "group"),
    )
    pairs = mesh.shape["group"] == 4 and mesh.shape["shard"] == 8
    return jax.shard_map(
        fast_device if pairs else on_device, mesh=mesh, in_specs=placed, out_specs=P(None, "shard", "group"), check_vma=False
    )
```
